32 devices in a mesh: obj: 16 (over z, x, core), ep: 2 (over y).
Axes of the slice: x: 2, y: 2, z: 4, core: 2. Of those that a mesh axis runs over, the one named last changes fastest.
Arguments:
- light_curves: float32 [2048, 256], P('obj', 'ep'), may hold values from -40 to 40
- valid: int32 [2048, 256], P('obj', 'ep'), may hold values 0 or 1
- pixel: int32 [2048], P('obj'), may hold values from 0 to 63, never falling along the last dimension, each value on 1 to 64 neighbouring positions
- inv_sigma: float32 [2048], P('obj'), may hold values from 0.5 to 4
- modes_init: float32 [256, 16], P('ep'), may hold values from -6 to 6
- epoch_jitter: float32 [256], replicated, may hold values from 0 to 0.9
- freq_index: int32 [2048], replicated, may hold values from 4 to 511
Outputs:
- residual: float32 [2048, 256], P('obj', 'ep')
- power: float32 [2048, 2048], P(('obj', 'ep'))
The draws below stay inside these ranges and needn't reach their ends.
Inputs may be any that keep to these rules, and one draw needn't show every extreme that they name: Pixels never decrease along the objects; each pixel holds 1 to 64 objects, and some pixel exactly 64.
All inputs are finite; a program needn't handle non-finite values. No bound on the sum of `valid` on one device may be relied on, other than what follows from the above.
Results may differ from the reference program's by a relative error of at most 0.0052.
Values may be sent and summed in bfloat16 or wider, within the bound.
A program may use at most 64 MiB of HBM per device.

```python
import math
import jax
import jax.numpy as jnp
import numpy as np
from jax import lax

K = 16
F = 2048
ITERS = 2
NOBJ = 2048
NEP = 256
NPIX = 64
MOST = 64
N_OBJ = 16


def draw_light_curves(key, part):
    key_strength = jax.random.fold_in(key, 101)
    key_amp = jax.random.fold_in(key, 102)
    key_mode = jax.random.fold_in(key, 103)
    key_noise = jax.random.fold_in(key, 104)
    key_jump = jax.random.fold_in(key, 105)
    key_size = jax.random.fold_in(key, 106)
    strength = jnp.exp(jax.random.uniform(key_strength, (K,), jnp.float32, math.log(0.3), math.log(3.0)))
    amplitude = jax.random.normal(key_amp, (NOBJ, K), jnp.float32) * strength[None, :]
    pattern = jax.random.normal(key_mode, (NEP, K), jnp.float32)
    trend = jnp.dot(amplitude, pattern.T, precision=lax.Precision.HIGHEST) * (1.5 / math.sqrt(K))
    noise = jax.random.normal(key_noise, (NOBJ, NEP), jnp.float32)
    jumps = jnp.where(jax.random.uniform(key_jump, (NOBJ, NEP), jnp.float32) < 0.02, 6.0 * jax.random.normal(key_size, (NOBJ, NEP), jnp.float32), 0.0)
    return jnp.clip(trend + noise + jumps, -40.0, 40.0).astype(jnp.float32)


def with_ends(drawn, rng, low, high):
    dims = drawn.shape
    spot = [jax.random.randint(jax.random.fold_in(rng, axis), (), 0, dims[axis]) for axis in range(len(dims))]
    drawn = drawn.at[tuple(spot)].set(low)
    longest = dims.index(max(dims))
    spot[longest] = (spot[longest] + 1) % dims[longest]
    return drawn.at[tuple(spot)].set(high)


def block_scale(own_key, dims, split, smallest, largest):
    loudness, own = 1.0, jax.random.fold_in(own_key, 6)
    for axis_at, blocks in split:
        steps = jnp.exp(jax.random.uniform(jax.random.fold_in(own, axis_at), (blocks,), jnp.float32, smallest / len(split), largest / len(split)))
        loudness = loudness * jnp.repeat(steps, dims[axis_at] // blocks).reshape([-1 if axis == axis_at else 1 for axis in range(len(dims))])
    return loudness


def split_up(amount, total, most, slope):
    loads = [(1 << 20) // math.isqrt(standing ** slope) + 1 for standing in range(2, amount + 1)]
    spare, holding = total - most - (amount - 1), [1] * (amount - 1)
    while spare > 0:
        candidates = [i for i in range(amount - 1) if holding[i] < most]
        mass, remaining = sum([loads[i] for i in candidates]), spare
        for i in candidates:
            extra = min(most - holding[i], max(1, remaining * loads[i] // mass), spare)
            holding[i] = holding[i] + extra
            spare = spare - extra
    return np.array([most] + holding)


def uneven(stream_key, amount, total, bound, lean):
    if amount == 2:
        one = jax.random.randint(stream_key, (), max(1, total - bound), min(bound, total - 1) + 1)
        return jnp.stack([one, total - one])
    lengths = jnp.asarray(split_up(amount, total, bound, lean), jnp.int32)
    twos = (amount - 1) // 2
    donor, receiver = lengths[1:1 + 2 * twos:2], lengths[2:2 + 2 * twos:2]
    margin = jnp.minimum(donor - 1, bound - receiver)
    shifted = jax.random.randint(jax.random.fold_in(stream_key, 1), (twos,), 0, 1 << 20) % (margin + 1)
    lengths = lengths.at[1:1 + 2 * twos:2].set(donor - shifted).at[2:2 + 2 * twos:2].set(receiver + shifted)
    return lengths[jax.random.permutation(jax.random.fold_in(stream_key, 2), amount)]


def bell_draw(rng, extent, deviation, most, cuts=(), held_as=jnp.bfloat16):
    factor_of = block_scale(rng, extent, cuts, -0.22, 0.18) if cuts else 1.0
    array = jax.random.normal(rng, extent, jnp.float32) * deviation * factor_of
    return jnp.minimum(jnp.maximum(array, -most), most).astype(held_as)


def setup_inputs(seed: int = 0) -> dict:
    key_of = jax.random.split(jax.random.key(seed), 8)
    return {
        "light_curves": draw_light_curves(jax.random.fold_in(key_of[7], 71), 0),
        "valid": with_ends((jax.random.randint(key_of[1], (NOBJ, NEP), 0, 4) < 3).astype(jnp.int32), jax.random.fold_in(key_of[1], 1), 0, 1),
        "pixel": jnp.searchsorted(jnp.cumsum(uneven(key_of[2], NPIX, NOBJ, MOST, 2)), jnp.arange(NOBJ), side="right").astype(jnp.int32),
        "inv_sigma": jnp.clip(jnp.exp(math.log(4.0) - 2.0794415 * jax.random.uniform(key_of[3], (NOBJ,), jnp.float32) ** block_scale(key_of[3], (NOBJ,), ((0, 16),), -0.2, 0.2)), 0.5, 4.0),
        "modes_init": bell_draw(key_of[4], (NEP, K), 1.0, 6.0, ((0, 2),), jnp.float32),
        "epoch_jitter": jnp.clip(jax.random.uniform(key_of[5], (NEP,), jnp.float32, 0.0, 0.9), 0.0, 0.9),
        "freq_index": with_ends(jax.random.randint(key_of[6], (F,), 4, 2 * NEP), jax.random.fold_in(key_of[6], 1), 4, (2 * NEP) - 1).astype(jnp.int32),
    }


HUBER = 1.345
DAMP = 2.0
RIDGE = 0.05
HIGHEST = lax.Precision.HIGHEST

def robust_weights(resid, mask_f, inv_sigma, pixel, npix):
    scaled = resid * inv_sigma[:, None]
    squares = lax.optimization_barrier(jnp.sum(mask_f * scaled * scaled, axis=1))
    valid_count = lax.optimization_barrier(jnp.sum(mask_f, axis=1))
    member = (pixel[None, :] == jnp.arange(npix, dtype=jnp.int32)[:, None]).astype(jnp.float32)
    sums = jnp.dot(member, squares, precision=HIGHEST)
    counts = jnp.dot(member, valid_count, precision=HIGHEST)
    spread = jnp.sqrt(sums / jnp.maximum(counts, 1.0) + 1e-06)
    object_spread = jnp.dot(spread, member, precision=HIGHEST)
    zscore = scaled / object_spread[:, None]
    huber = HUBER / jnp.maximum(jnp.abs(zscore), HUBER)
    return mask_f * huber * (inv_sigma * inv_sigma)[:, None]

def damped_solve(gram, target):
    order = target.shape[1]
    identity = jnp.eye(order, dtype=gram.dtype)
    return jnp.linalg.solve(gram + DAMP * identity, target[..., None])[..., 0]

def spectrum_sums(weighted, weight, times, freqs):
    cycles = times[:, None] * freqs[None, :]
    angle = 2.0 * math.pi * (cycles - jnp.floor(cycles))
    basis = jnp.concatenate([jnp.cos(angle), jnp.sin(angle), jnp.cos(2.0 * angle), jnp.sin(2.0 * angle)], axis=1).astype(jnp.bfloat16)
    width = freqs.shape[0]
    by_weight = jnp.dot(weight.astype(jnp.float32), basis.astype(jnp.float32), preferred_element_type=jnp.float32)
    by_value = jnp.dot(weighted.astype(jnp.float32), basis[:, :2 * width].astype(jnp.float32), preferred_element_type=jnp.float32)
    return (by_weight, by_value)

def powers(by_weight, by_value, total, level):
    width = by_value.shape[1] // 2
    cosine = by_weight[:, :width]
    sine = by_weight[:, width:2 * width]
    cosine_two = by_weight[:, 2 * width:3 * width]
    sine_two = by_weight[:, 3 * width:]
    mean_level = level / total
    ycos = by_value[:, :width] - mean_level * cosine
    ysin = by_value[:, width:] - mean_level * sine
    cc_term = 0.5 * (total + cosine_two) - cosine * cosine / total + RIDGE * total
    ss_term = 0.5 * (total - cosine_two) - sine * sine / total + RIDGE * total
    cs_term = 0.5 * sine_two - cosine * sine / total
    determinant = cc_term * ss_term - cs_term * cs_term
    return (ss_term * ycos * ycos + cc_term * ysin * ysin - 2.0 * cs_term * ycos * ysin) / determinant

def reference(light_curves, valid, pixel, inv_sigma, modes_init, epoch_jitter, freq_index):
    npix = 4 * N_OBJ
    mask_f = valid.astype(jnp.float32)
    modes = modes_init
    coef = jnp.zeros((NOBJ, K), jnp.float32)
    for iteration in range(ITERS):
        resid = light_curves - jnp.dot(coef, modes.T, precision=HIGHEST)
        weight = robust_weights(resid, mask_f, inv_sigma, pixel, npix)
        outer = (modes[:, :, None] * modes[:, None, :]).reshape(NEP, K * K)
        gram = jnp.dot(weight, outer, precision=HIGHEST).reshape(NOBJ, K, K)
        target = jnp.dot(weight * light_curves, modes, precision=HIGHEST)
        coef = damped_solve(gram, target)
        resid = light_curves - jnp.dot(coef, modes.T, precision=HIGHEST)
        weight = robust_weights(resid, mask_f, inv_sigma, pixel, npix)
        outer = (coef[:, :, None] * coef[:, None, :]).reshape(NOBJ, K * K)
        gram = jnp.dot(weight.T, outer, precision=HIGHEST).reshape(NEP, K, K)
        target = jnp.dot((weight * light_curves).T, coef, precision=HIGHEST)
        modes = damped_solve(gram, target)
    residual = light_curves - jnp.dot(coef, modes.T, precision=HIGHEST)
    final_weight = robust_weights(residual, mask_f, inv_sigma, pixel, npix)
    weighted = (final_weight * residual).astype(jnp.bfloat16)
    weight_b = final_weight.astype(jnp.bfloat16)
    total = lax.optimization_barrier(jnp.sum(weight_b, axis=1, keepdims=True, dtype=jnp.float32))
    level = lax.optimization_barrier(jnp.sum(weighted, axis=1, keepdims=True, dtype=jnp.float32))
    times = jnp.arange(NEP, dtype=jnp.int32).astype(jnp.float32) + epoch_jitter
    freqs = (freq_index + 1).astype(jnp.float32) / (4.0 * NEP)
    size = math.gcd(F, 512)
    blocks = freqs.reshape(F // size, size)

    def one_block(block_freqs):
        by_weight, by_value = spectrum_sums(weighted, weight_b, times, block_freqs)
        return powers(by_weight, by_value, total, level)
    power = lax.map(one_block, blocks)
    power = jnp.transpose(power, (1, 0, 2)).reshape(NOBJ, F)
    return (residual, power)
```

```python
import functools
import math

import jax
import jax.numpy as jnp
from jax import lax
from jax.experimental import pallas as pl
from jax.experimental.pallas import tpu as pltpu
from jax.sharding import PartitionSpec as P

ITERS = 2


HUBER = 1.345
DAMP = 2.0
RIDGE = 0.05
HIGHEST = lax.Precision.HIGHEST
LANES = 128
SUB = 8
F32 = jnp.float32
MESH = pl.DeviceIdType.MESH


def first_of(row):
    return SUB * (row // SUB)


def packed_outer(vectors):
    order = vectors.shape[0]
    return jnp.concatenate(
        [vectors[i : i + 1] * vectors[first_of(i) :] for i in range(order)], axis=0
    )


def damped_solve(packed, order):
    level = lax.broadcasted_iota(jnp.int32, (order, packed.shape[1]), 0)
    rows = []
    at = 0
    for i in range(order):
        low = first_of(i)
        rows.append(packed[at : at + order - low] + DAMP * (level[low:] == i).astype(F32))
        at += order - low
    remain = packed[at : at + order]
    inverse, forward = [], []
    for k in range(order):
        low = first_of(k)
        row = rows[k]
        inverse.append(1.0 / row[k - low : k - low + 1])
        scaled = row * inverse[k]
        for j in range(k + 1, order):
            begin = first_of(j)
            rows[j] = rows[j] - scaled[j - low : j - low + 1] * row[begin - low :]
        forward.append(remain[k : k + 1])
        part = remain[low:] - scaled * forward[k]
        remain = part if low == 0 else jnp.concatenate([remain[:low], part], axis=0)
    solved = jnp.zeros((order, packed.shape[1]), F32)
    for k in reversed(range(order)):
        low = first_of(k)
        known = jnp.sum(rows[k] * solved[low:], axis=0, keepdims=True)
        value = (forward[k] - known) * inverse[k]
        solved = jnp.where(level == k, value, solved)
    return solved


def spread_out(values, rows, cols):
    down, right = rows - values.shape[0], cols - values.shape[1]
    return jnp.pad(values, ((0, down), (0, right)))


def detrend_kernel(
    obj_n, ep_n, order, near, lc_ref, valid_ref, pixel_ref, sigma_ref, modes_ref,
    resid_ref, wq_ref, wb_ref,
    coef_s, modes_s, pix_send, pix_recv, ep_send, ep_recv, gram_send, gram_recv,
    mode_send, mode_recv, half_send, half_recv,
    pix_sem, ep_sem, gram_sem, mode_sem, half_sem,
):
    me_o, me_e = lax.axis_index("obj"), lax.axis_index("ep")
    rows, cols = lc_ref.shape
    blocks = cols // SUB
    share = rows // ep_n

    def device(do, de):
        return {
            "obj": lax.rem(me_o + do, obj_n),
            "ep": lax.rem(me_e + de, ep_n),
        }

    peers = list(near)
    peers += [(do, 0) for do in range(1, obj_n) if (do, 0) not in near]
    barrier = pltpu.get_barrier_semaphore()
    for do, de in peers:
        pl.semaphore_signal(barrier, inc=1, device_id=device(do, de), device_id_type=MESH)
    pl.semaphore_wait(barrier, len(peers))

    mask = valid_ref[...].astype(F32)
    sigma = sigma_ref[...]
    pixels = lax.broadcasted_iota(jnp.int32, (rows, pix_send.shape[2]), 1)
    member = (pixel_ref[...] == pixels).astype(F32)
    counts = jnp.sum(member * jnp.sum(mask, axis=1, keepdims=True), axis=0, keepdims=True)

    def residual():
        return lc_ref[...] - lax.dot_general(
            coef_s[...], modes_s[...], (((0,), (0,)), ((), ())),
            precision=HIGHEST, preferred_element_type=F32,
        )

    def robust(resid, phase):
        scaled = resid * sigma
        squares = jnp.sum(mask * scaled * scaled, axis=1, keepdims=True)
        sums = jnp.sum(member * squares, axis=0, keepdims=True)
        part = spread_out(jnp.concatenate([sums, counts], axis=0), SUB, sums.shape[1])
        pix_send[phase] = part
        copies = []
        for k, (do, de) in enumerate(near):
            copies.append(pltpu.make_async_remote_copy(
                src_ref=pix_send.at[phase], dst_ref=pix_recv.at[phase, k],
                send_sem=pix_sem.at[0, phase, k], recv_sem=pix_sem.at[1, phase, k],
                device_id=device(do, de), device_id_type=MESH,
            ))
            copies[k].start()
        for copy in copies:
            copy.wait()
        totals = part
        for k in range(len(near)):
            totals = totals + pix_recv[phase, k]
        spread = jnp.sqrt(totals[0:1] / jnp.maximum(totals[1:2], 1.0) + 1e-06)
        object_spread = jnp.sum(member * spread, axis=1, keepdims=True)
        zscore = scaled / object_spread
        huber = HUBER / jnp.maximum(jnp.abs(zscore), HUBER)
        return mask * huber * (sigma * sigma)

    coef_s[...] = jnp.zeros_like(coef_s)
    modes_s[...] = modes_ref[...]

    def iteration(it, carry):
        light = lc_ref[...]
        weight = robust(residual(), 2 * it)
        modes_t = modes_s[...]
        last = (((1,), (1,)), ((), ()))
        gram = lax.dot_general(
            packed_outer(modes_t), weight, last, precision=HIGHEST, preferred_element_type=F32
        )
        target = lax.dot_general(
            modes_t, weight * light, last, precision=HIGHEST, preferred_element_type=F32
        )
        packed = jnp.concatenate([gram, target], axis=0)
        ep_send[it] = packed
        copies = []
        for k in range(1, ep_n):
            copies.append(pltpu.make_async_remote_copy(
                src_ref=ep_send.at[it], dst_ref=ep_recv.at[it, k - 1],
                send_sem=ep_sem.at[0, it, k - 1], recv_sem=ep_sem.at[1, it, k - 1],
                device_id=device(0, k), device_id_type=MESH,
            ))
            copies[-1].start()
        for k in range(1, ep_n):
            copies[k - 1].wait()
            packed = packed + ep_recv[it, k - 1]
        coef_t = damped_solve(packed, order)
        coef_s[...] = coef_t

        weight = robust(residual(), 2 * it + 1)
        gram = jnp.dot(
            packed_outer(coef_t), weight, precision=HIGHEST, preferred_element_type=F32
        )
        target = jnp.dot(
            coef_t, weight * light, precision=HIGHEST, preferred_element_type=F32
        )
        packed = jnp.concatenate([gram, target], axis=0)
        depth = packed.shape[0]
        wide = gram_send.shape[3]
        turned = spread_out(packed, wide, cols).T
        gram_send[it] = turned.reshape(blocks, SUB, wide)
        copies = []
        for k in range(1, obj_n):
            there = lax.rem(me_o + k, obj_n)
            copies.append(pltpu.make_async_remote_copy(
                src_ref=gram_send.at[it, lax.rem(there, blocks)],
                dst_ref=gram_recv.at[it, k - 1],
                send_sem=gram_sem.at[0, it, k - 1], recv_sem=gram_sem.at[1, it, k - 1],
                device_id=device(k, 0), device_id_type=MESH,
            ))
            copies[-1].start()
        total = gram_send[it, lax.rem(me_o, blocks)]
        for k in range(1, obj_n):
            copies[k - 1].wait()
            total = total + gram_recv[it, k - 1]
        packed = spread_out(total, LANES, wide).T[:depth]
        solved = damped_solve(packed, order)
        mine = spread_out(solved, LANES, LANES).T[:SUB]
        mode_send[it] = mine
        mode_recv[it, me_o] = mine
        copies = []
        for k in range(1, obj_n):
            copies.append(pltpu.make_async_remote_copy(
                src_ref=mode_send.at[it], dst_ref=mode_recv.at[it, me_o],
                send_sem=mode_sem.at[0, it, k - 1], recv_sem=mode_sem.at[1, it, k - 1],
                device_id=device(k, 0), device_id_type=MESH,
            ))
            copies[-1].start()
        for copy in copies:
            copy.wait()
        modes_s[...] = mode_recv[it, :blocks].reshape(cols, LANES).T[:order]
        return carry

    lax.fori_loop(0, ITERS, iteration, 0)
    resid = residual()
    resid_ref[...] = resid
    weight = robust(resid, 2 * ITERS)
    half_send[0] = (weight * resid).astype(jnp.bfloat16)
    half_send[1] = weight.astype(jnp.bfloat16)
    copies = []
    for k in range(1, ep_n):
        there = lax.rem(me_e + k, ep_n)
        copies.append(pltpu.make_async_remote_copy(
            src_ref=half_send.at[:, pl.ds(pl.multiple_of(there * share, share), share), :],
            dst_ref=half_recv.at[me_e],
            send_sem=half_sem.at[0, k - 1], recv_sem=half_sem.at[1, k - 1],
            device_id=device(0, k), device_id_type=MESH,
        ))
        copies[-1].start()
    half_recv[me_e] = half_send[:, pl.ds(pl.multiple_of(me_e * share, share), share), :]
    for copy in copies:
        copy.wait()
    for e in range(ep_n):
        wq_ref[:, e * cols : (e + 1) * cols] = half_recv[e, 0]
        wb_ref[:, e * cols : (e + 1) * cols] = half_recv[e, 1]


SIN_TERMS = [(-1.0) ** n / math.factorial(2 * n + 1) for n in range(7)]
COS_TERMS = [(-1.0) ** n / math.factorial(2 * n) for n in range(8)]


def series(square, terms):
    value = jnp.full_like(square, terms[-1])
    for term in terms[-2::-1]:
        value = value * square + term
    return value


def power_kernel(wq_ref, wb_ref, times_ref, freqs_ref, power_ref):
    values, weights = wq_ref[...], wb_ref[...]
    total = jnp.sum(weights.astype(F32), axis=1, keepdims=True)
    level = jnp.sum(values.astype(F32), axis=1, keepdims=True)
    cycles = times_ref[...] * freqs_ref[...]
    cycles = cycles - jnp.floor(cycles)
    turn = jnp.where(cycles >= 0.5, cycles - 1.0, cycles)
    angle = (2.0 * math.pi) * (jnp.abs(turn) - 0.25)
    square = angle * angle
    cos_b = -angle * series(square, SIN_TERMS)
    size = series(square, COS_TERMS)
    sin_b = jnp.where(turn < 0.0, -size, size)

    def sums(rows, basis):
        return jnp.dot(rows, basis.astype(jnp.bfloat16), preferred_element_type=F32)

    both = jnp.concatenate([weights, values], axis=0)
    count = weights.shape[0]
    by_cos = sums(both, cos_b)
    by_sin = sums(both, sin_b)
    cosine, sine = by_cos[:count], by_sin[:count]
    cosine_two = sums(weights, 2.0 * cos_b * cos_b - 1.0)
    sine_two = sums(weights, 2.0 * sin_b * cos_b)
    inverse = 1.0 / total
    mean_level = level * inverse
    ycos = by_cos[count:] - mean_level * cosine
    ysin = by_sin[count:] - mean_level * sine
    cc_term = 0.5 * (total + cosine_two) - cosine * cosine * inverse + RIDGE * total
    ss_term = 0.5 * (total - cosine_two) - sine * sine * inverse + RIDGE * total
    cs_term = 0.5 * sine_two - cosine * sine * inverse
    determinant = cc_term * ss_term - cs_term * cs_term
    power_ref[...] = (
        ss_term * ycos * ycos + cc_term * ysin * ysin - 2.0 * cs_term * ycos * ysin
    ) / determinant


def per_device(light_curves, valid, pixel, inv_sigma, modes_init, epoch_jitter, freq_index):
    obj_n = lax.axis_size("obj")
    ep_n = lax.axis_size("ep")
    order = modes_init.shape[1]
    rows, cols = light_curves.shape
    share = rows // ep_n
    epochs = epoch_jitter.shape[0]
    pix_lanes = -(-4 * obj_n // LANES) * LANES
    near = [
        (do, de)
        for do in sorted({0, 1 % obj_n, (obj_n - 1) % obj_n})
        for de in range(ep_n)
        if (do, de) != (0, 0)
    ]
    depth = sum(order - first_of(i) for i in range(order)) + order
    wide = -(-depth // LANES) * LANES
    phases = 2 * ITERS + 1
    vmem = pl.BlockSpec(memory_space=pltpu.VMEM)
    sem = pltpu.SemaphoreType.DMA
    residual, values, weights = pl.pallas_call(
        functools.partial(detrend_kernel, obj_n, ep_n, order, near),
        out_shape=(
            jax.ShapeDtypeStruct((rows, cols), F32),
            jax.ShapeDtypeStruct((share, epochs), jnp.bfloat16),
            jax.ShapeDtypeStruct((share, epochs), jnp.bfloat16),
        ),
        in_specs=[vmem] * 5,
        out_specs=(vmem,) * 3,
        scratch_shapes=[
            pltpu.VMEM((order, rows), F32),
            pltpu.VMEM((order, cols), F32),
            pltpu.VMEM((phases, SUB, pix_lanes), F32),
            pltpu.VMEM((phases, len(near), SUB, pix_lanes), F32),
            pltpu.VMEM((ITERS, depth, rows), F32),
            pltpu.VMEM((ITERS, max(ep_n - 1, 1), depth, rows), F32),
            pltpu.VMEM((ITERS, cols // SUB, SUB, wide), F32),
            pltpu.VMEM((ITERS, max(obj_n - 1, 1), SUB, wide), F32),
            pltpu.VMEM((ITERS, SUB, LANES), F32),
            pltpu.VMEM((ITERS, max(obj_n, cols // SUB), SUB, LANES), F32),
            pltpu.VMEM((2, rows, cols), jnp.bfloat16),
            pltpu.VMEM((ep_n, 2, share, cols), jnp.bfloat16),
            sem((2, phases, len(near))),
            sem((2, ITERS, max(ep_n - 1, 1))),
            sem((2, ITERS, max(obj_n - 1, 1))),
            sem((2, ITERS, max(obj_n - 1, 1))),
            sem((2, max(ep_n - 1, 1))),
        ],
        compiler_params=pltpu.CompilerParams(collective_id=0, has_side_effects=True),
    )(light_curves, valid, pixel[:, None], inv_sigma[:, None], modes_init.T)

    times = jnp.arange(epochs, dtype=jnp.int32).astype(F32) + epoch_jitter
    freqs = (freq_index + 1).astype(F32) / (4.0 * epochs)
    count = freqs.shape[0]
    size = math.gcd(count, 256)
    whole = lambda shape: pl.BlockSpec(shape, lambda i: (0, 0))
    power = pl.pallas_call(
        power_kernel,
        grid=(count // size,),
        out_shape=jax.ShapeDtypeStruct((share, count), F32),
        in_specs=[
            whole((share, epochs)),
            whole((share, epochs)),
            whole((epochs, 1)),
            pl.BlockSpec((1, size), lambda i: (0, i)),
        ],
        out_specs=pl.BlockSpec((share, size), lambda i: (0, i)),
    )(values, weights, times[:, None], freqs[None, :])
    return (residual, power)


def solution(mesh):
    in_specs = (P("obj", "ep"), P("obj", "ep"), P("obj"), P("obj"), P("ep", None), P(), P())
    out_specs = (P("obj", "ep"), P(("obj", "ep"), None))
    return jax.shard_map(
        per_device, mesh=mesh, in_specs=in_specs, out_specs=out_specs, check_vma=False
    )
```

```python
import functools
import math

import jax
import jax.numpy as jnp
from jax import lax
from jax.experimental import pallas as pl
from jax.experimental.pallas import tpu as pltpu
from jax.sharding import PartitionSpec as P

ITERS = 2


HUBER = 1.345
DAMP = 2.0
RIDGE = 0.05
HIGHEST = lax.Precision.HIGHEST
LANES = 128
SUB = 8
F32 = jnp.float32
STRIP = 32
MESH = pl.DeviceIdType.MESH


def first_of(row):
    return SUB * (row // SUB)


def packed_outer(vectors):
    order = vectors.shape[0]
    return jnp.concatenate(
        [vectors[i : i + 1] * vectors[first_of(i) :] for i in range(order)], axis=0
    )


def damped_solve(packed, order):
    level = lax.broadcasted_iota(jnp.int32, (order, packed.shape[1]), 0)
    rows = []
    at = 0
    for i in range(order):
        low = first_of(i)
        rows.append(packed[at : at + order - low] + DAMP * (level[low:] == i).astype(F32))
        at += order - low
    remain = packed[at : at + order]
    inverse, forward = [], []
    for k in range(order):
        low = first_of(k)
        row = rows[k]
        inverse.append(1.0 / row[k - low : k - low + 1])
        scaled = row * inverse[k]
        for j in range(k + 1, order):
            begin = first_of(j)
            rows[j] = rows[j] - scaled[j - low : j - low + 1] * row[begin - low :]
        forward.append(remain[k : k + 1])
        part = remain[low:] - scaled * forward[k]
        remain = part if low == 0 else jnp.concatenate([remain[:low], part], axis=0)
    solved = jnp.zeros((order, packed.shape[1]), F32)
    for k in reversed(range(order)):
        low = first_of(k)
        known = jnp.sum(rows[k] * solved[low:], axis=0, keepdims=True)
        value = (forward[k] - known) * inverse[k]
        solved = jnp.where(level == k, value, solved)
    return solved


def spread_out(values, rows, cols):
    down, right = rows - values.shape[0], cols - values.shape[1]
    return jnp.pad(values, ((0, down), (0, right)))


def as_column(row):
    return jnp.broadcast_to(row, (LANES, row.shape[1])).T


def detrend_kernel(
    obj_n, ep_n, order, near, lc_ref, valid_ref, pixel_ref, sigma_ref, modes_ref,
    jitter_ref, freq_ref, resid_ref, power_ref, basis_s, times_s,
    coef_s, modes_s, pix_send, pix_recv, ep_send, ep_recv, gram_send, gram_recv,
    mode_send, mode_recv, half_send, half_recv,
    pix_sem, ep_sem, gram_sem, mode_sem, half_sem,
):
    me_o, me_e = lax.axis_index("obj"), lax.axis_index("ep")
    rows, cols = lc_ref.shape
    blocks = cols // SUB
    share = rows // ep_n

    def device(do, de):
        return {
            "obj": lax.rem(me_o + do, obj_n),
            "ep": lax.rem(me_e + de, ep_n),
        }

    peers = list(near)
    peers += [(do, 0) for do in range(1, obj_n) if (do, 0) not in near]
    barrier = pltpu.get_barrier_semaphore()
    for do, de in peers:
        pl.semaphore_signal(barrier, inc=1, device_id=device(do, de), device_id_type=MESH)
    pl.semaphore_wait(barrier, len(peers))

    mask = valid_ref[...].astype(F32)
    sigma = as_column(sigma_ref[...])[:, :1]
    epochs = jitter_ref.shape[1]
    times_s[...] = as_column(
        lax.broadcasted_iota(jnp.int32, (1, epochs), 1).astype(F32) + jitter_ref[...]
    )
    width = basis_s.shape[3]

    def fill_basis(block):
        begin = pl.multiple_of(block * width, width)
        freqs = (freq_ref[:, pl.ds(begin, width)] + 1).astype(F32) / (4.0 * epochs)

        def strip(step, carry):
            at = pl.ds(pl.multiple_of(step * STRIP, STRIP), STRIP)
            times = jnp.concatenate([times_s[at, :]] * (width // LANES), axis=1)
            for kind, values in enumerate(basis_of(times * freqs)):
                basis_s[block, kind, at, :] = values.astype(jnp.bfloat16)
            return carry

        lax.fori_loop(0, epochs // STRIP, strip, 0)

    pixels = lax.broadcasted_iota(jnp.int32, (rows, pix_send.shape[2]), 1)
    member = (as_column(pixel_ref[...].astype(F32))[:, :1] == pixels.astype(F32)).astype(F32)
    counts = jnp.sum(member * jnp.sum(mask, axis=1, keepdims=True), axis=0, keepdims=True)

    def residual():
        return lc_ref[...] - lax.dot_general(
            coef_s[...], modes_s[...], (((0,), (0,)), ((), ())),
            precision=HIGHEST, preferred_element_type=F32,
        )

    def robust(resid, phase, block=None):
        scaled = resid * sigma
        squares = jnp.sum(mask * scaled * scaled, axis=1, keepdims=True)
        sums = jnp.sum(member * squares, axis=0, keepdims=True)
        part = spread_out(jnp.concatenate([sums, counts], axis=0), SUB, sums.shape[1])
        pix_send[phase] = part
        copies = []
        for k, (do, de) in enumerate(near):
            copies.append(pltpu.make_async_remote_copy(
                src_ref=pix_send.at[phase], dst_ref=pix_recv.at[phase, k],
                send_sem=pix_sem.at[0, phase, k], recv_sem=pix_sem.at[1, phase, k],
                device_id=device(do, de), device_id_type=MESH,
            ))
            copies[k].start()
        if block is not None:
            fill_basis(block)
        for copy in copies:
            copy.wait()
        totals = part
        for k in range(len(near)):
            totals = totals + pix_recv[phase, k]
        spread = jnp.sqrt(totals[0:1] / jnp.maximum(totals[1:2], 1.0) + 1e-06)
        object_spread = jnp.sum(member * spread, axis=1, keepdims=True)
        zscore = scaled / object_spread
        huber = HUBER / jnp.maximum(jnp.abs(zscore), HUBER)
        return mask * huber * (sigma * sigma)

    coef_s[...] = jnp.zeros_like(coef_s)
    modes_s[...] = spread_out(modes_ref[...], cols, LANES).T[:order]

    def iteration(it, carry):
        light = lc_ref[...]
        weight = robust(residual(), 2 * it, 4 * it)
        modes_t = modes_s[...]
        last = (((1,), (1,)), ((), ()))
        gram = lax.dot_general(
            packed_outer(modes_t), weight, last, precision=HIGHEST, preferred_element_type=F32
        )
        target = lax.dot_general(
            modes_t, weight * light, last, precision=HIGHEST, preferred_element_type=F32
        )
        packed = jnp.concatenate([gram, target], axis=0)
        ep_send[it] = packed
        copies = []
        for k in range(1, ep_n):
            copies.append(pltpu.make_async_remote_copy(
                src_ref=ep_send.at[it], dst_ref=ep_recv.at[it, k - 1],
                send_sem=ep_sem.at[0, it, k - 1], recv_sem=ep_sem.at[1, it, k - 1],
                device_id=device(0, k), device_id_type=MESH,
            ))
            copies[-1].start()
        for k in range(1, ep_n):
            copies[k - 1].wait()
            packed = packed + ep_recv[it, k - 1]
        coef_t = damped_solve(packed, order)
        coef_s[...] = coef_t

        weight = robust(residual(), 2 * it + 1, 4 * it + 1)
        gram = jnp.dot(
            packed_outer(coef_t), weight, precision=HIGHEST, preferred_element_type=F32
        )
        target = jnp.dot(
            coef_t, weight * light, precision=HIGHEST, preferred_element_type=F32
        )
        packed = jnp.concatenate([gram, target], axis=0)
        depth = packed.shape[0]
        wide = gram_send.shape[3]
        turned = spread_out(packed, wide, cols).T
        gram_send[it] = turned.reshape(blocks, SUB, wide)
        copies = []
        for k in range(1, obj_n):
            there = lax.rem(me_o + k, obj_n)
            copies.append(pltpu.make_async_remote_copy(
                src_ref=gram_send.at[it, lax.rem(there, blocks)],
                dst_ref=gram_recv.at[it, k - 1],
                send_sem=gram_sem.at[0, it, k - 1], recv_sem=gram_sem.at[1, it, k - 1],
                device_id=device(k, 0), device_id_type=MESH,
            ))
            copies[-1].start()
        fill_basis(4 * it + 2)
        total = gram_send[it, lax.rem(me_o, blocks)]
        for k in range(1, obj_n):
            copies[k - 1].wait()
            total = total + gram_recv[it, k - 1]
        packed = spread_out(total, LANES, wide).T[:depth]
        solved = damped_solve(packed, order)
        mine = spread_out(solved, LANES, LANES).T[:SUB]
        mode_send[it] = mine
        mode_recv[it, me_o] = mine
        copies = []
        for k in range(1, obj_n):
            copies.append(pltpu.make_async_remote_copy(
                src_ref=mode_send.at[it], dst_ref=mode_recv.at[it, me_o],
                send_sem=mode_sem.at[0, it, k - 1], recv_sem=mode_sem.at[1, it, k - 1],
                device_id=device(k, 0), device_id_type=MESH,
            ))
            copies[-1].start()
        fill_basis(4 * it + 3)
        for copy in copies:
            copy.wait()
        modes_s[...] = mode_recv[it, :blocks].reshape(cols, LANES).T[:order]
        return carry

    lax.fori_loop(0, ITERS, iteration, 0)
    resid = residual()
    resid_ref[...] = resid
    weight = robust(resid, 2 * ITERS)
    half_send[0] = (weight * resid).astype(jnp.bfloat16)
    half_send[1] = weight.astype(jnp.bfloat16)
    copies = []
    for k in range(1, ep_n):
        there = lax.rem(me_e + k, ep_n)
        copies.append(pltpu.make_async_remote_copy(
            src_ref=half_send.at[:, pl.ds(pl.multiple_of(there * share, share), share), :],
            dst_ref=half_recv.at[me_e],
            send_sem=half_sem.at[0, k - 1], recv_sem=half_sem.at[1, k - 1],
            device_id=device(0, k), device_id_type=MESH,
        ))
        copies[-1].start()
    half_recv[me_e] = half_send[:, pl.ds(pl.multiple_of(me_e * share, share), share), :]
    for copy in copies:
        copy.wait()
    received = [half_recv[e] for e in range(ep_n)]
    values = jnp.concatenate([half[0] for half in received], axis=1)
    weights = jnp.concatenate([half[1] for half in received], axis=1)
    both = jnp.concatenate([weights, values], axis=0)
    total = jnp.sum(weights.astype(F32), axis=1, keepdims=True)
    level = jnp.sum(values.astype(F32), axis=1, keepdims=True)

    def spectrum(block, carry):
        at = pl.ds(pl.multiple_of(block * width, width), width)
        power_ref[:, at] = powers(
            jnp.dot(both, basis_s[block, 0], preferred_element_type=F32),
            jnp.dot(both, basis_s[block, 1], preferred_element_type=F32),
            jnp.dot(weights, basis_s[block, 2], preferred_element_type=F32),
            jnp.dot(weights, basis_s[block, 3], preferred_element_type=F32),
            total,
            level,
        )
        return carry

    lax.fori_loop(0, basis_s.shape[0], spectrum, 0)


SIN_TERMS = [(-1.0) ** n / math.factorial(2 * n + 1) for n in range(7)]
COS_TERMS = [(-1.0) ** n / math.factorial(2 * n) for n in range(8)]


def series(square, terms):
    value = jnp.full_like(square, terms[-1])
    for term in terms[-2::-1]:
        value = value * square + term
    return value


def basis_of(cycles):
    cycles = cycles - jnp.floor(cycles)
    turn = jnp.where(cycles >= 0.5, cycles - 1.0, cycles)
    angle = (2.0 * math.pi) * (jnp.abs(turn) - 0.25)
    square = angle * angle
    cosine = -angle * series(square, SIN_TERMS)
    size = series(square, COS_TERMS)
    sine = jnp.where(turn < 0.0, -size, size)
    return cosine, sine, 2.0 * cosine * cosine - 1.0, 2.0 * sine * cosine


def powers(by_cos, by_sin, cosine_two, sine_two, total, level):
    count = cosine_two.shape[0]
    cosine, sine = by_cos[:count], by_sin[:count]
    inverse = 1.0 / total
    mean_level = level * inverse
    ycos = by_cos[count:] - mean_level * cosine
    ysin = by_sin[count:] - mean_level * sine
    cc_term = 0.5 * (total + cosine_two) - cosine * cosine * inverse + RIDGE * total
    ss_term = 0.5 * (total - cosine_two) - sine * sine * inverse + RIDGE * total
    cs_term = 0.5 * sine_two - cosine * sine * inverse
    determinant = cc_term * ss_term - cs_term * cs_term
    return (
        ss_term * ycos * ycos + cc_term * ysin * ysin - 2.0 * cs_term * ycos * ysin
    ) / determinant


def per_device(light_curves, valid, pixel, inv_sigma, modes_init, epoch_jitter, freq_index):
    obj_n = lax.axis_size("obj")
    ep_n = lax.axis_size("ep")
    order = modes_init.shape[1]
    rows, cols = light_curves.shape
    share = rows // ep_n
    epochs = epoch_jitter.shape[0]
    pix_lanes = -(-4 * obj_n // LANES) * LANES
    near = [
        (do, de)
        for do in sorted({0, 1 % obj_n, (obj_n - 1) % obj_n})
        for de in range(ep_n)
        if (do, de) != (0, 0)
    ]
    depth = sum(order - first_of(i) for i in range(order)) + order
    wide = -(-depth // LANES) * LANES
    phases = 2 * ITERS + 1
    vmem = pl.BlockSpec(memory_space=pltpu.VMEM)
    sem = pltpu.SemaphoreType.DMA
    count = freq_index.shape[0]
    parts = 4 * ITERS
    return pl.pallas_call(
        functools.partial(detrend_kernel, obj_n, ep_n, order, near),
        out_shape=(
            jax.ShapeDtypeStruct((rows, cols), F32),
            jax.ShapeDtypeStruct((share, count), F32),
        ),
        in_specs=[vmem] * 7,
        out_specs=(vmem,) * 2,
        scratch_shapes=[
            pltpu.VMEM((parts, 4, epochs, count // parts), jnp.bfloat16),
            pltpu.VMEM((epochs, LANES), F32),
            pltpu.VMEM((order, rows), F32),
            pltpu.VMEM((order, cols), F32),
            pltpu.VMEM((phases, SUB, pix_lanes), F32),
            pltpu.VMEM((phases, len(near), SUB, pix_lanes), F32),
            pltpu.VMEM((ITERS, depth, rows), F32),
            pltpu.VMEM((ITERS, max(ep_n - 1, 1), depth, rows), F32),
            pltpu.VMEM((ITERS, cols // SUB, SUB, wide), F32),
            pltpu.VMEM((ITERS, max(obj_n - 1, 1), SUB, wide), F32),
            pltpu.VMEM((ITERS, SUB, LANES), F32),
            pltpu.VMEM((ITERS, max(obj_n, cols // SUB), SUB, LANES), F32),
            pltpu.VMEM((2, rows, cols), jnp.bfloat16),
            pltpu.VMEM((ep_n, 2, share, cols), jnp.bfloat16),
            sem((2, phases, len(near))),
            sem((2, ITERS, max(ep_n - 1, 1))),
            sem((2, ITERS, max(obj_n - 1, 1))),
            sem((2, ITERS, max(obj_n - 1, 1))),
            sem((2, max(ep_n - 1, 1))),
        ],
        compiler_params=pltpu.CompilerParams(collective_id=0, has_side_effects=True),
    )(
        light_curves, valid, pixel[None], inv_sigma[None], modes_init,
        epoch_jitter[None], freq_index[None],
    )


def solution(mesh):
    in_specs = (P("obj", "ep"), P("obj", "ep"), P("obj"), P("obj"), P("ep", None), P(), P())
    out_specs = (P("obj", "ep"), P(("obj", "ep"), None))
    return jax.shard_map(
        per_device, mesh=mesh, in_specs=in_specs, out_specs=out_specs, check_vma=False
    )
```

```python
import functools
import math

import jax
import jax.numpy as jnp
from jax import lax
from jax.experimental import pallas as pl
from jax.experimental.pallas import tpu as pltpu
from jax.sharding import PartitionSpec as P

ITERS = 2


HUBER = 1.345
DAMP = 2.0
RIDGE = 0.05
HIGHEST = lax.Precision.HIGHEST
LANES = 128
SUB = 8
F32 = jnp.float32
STRIP = 32
MESH = pl.DeviceIdType.MESH


def first_of(row):
    return SUB * (row // SUB)


def packed_outer(vectors):
    order = vectors.shape[0]
    return jnp.concatenate(
        [vectors[i : i + 1] * vectors[first_of(i) :] for i in range(order)], axis=0
    )


def damped_solve(packed, order):
    level = lax.broadcasted_iota(jnp.int32, (order, packed.shape[1]), 0)
    rows = []
    at = 0
    for i in range(order):
        low = first_of(i)
        rows.append(packed[at : at + order - low] + DAMP * (level[low:] == i).astype(F32))
        at += order - low
    remain = packed[at : at + order]
    inverse, forward = [], []
    for k in range(order):
        low = first_of(k)
        row = rows[k]
        inverse.append(1.0 / row[k - low : k - low + 1])
        scaled = row * inverse[k]
        for j in range(k + 1, order):
            begin = first_of(j)
            rows[j] = rows[j] - scaled[j - low : j - low + 1] * row[begin - low :]
        forward.append(remain[k : k + 1])
        part = remain[low:] - scaled * forward[k]
        remain = part if low == 0 else jnp.concatenate([remain[:low], part], axis=0)
    solved = jnp.zeros((order, packed.shape[1]), F32)
    for k in reversed(range(order)):
        low = first_of(k)
        known = jnp.sum(rows[k] * solved[low:], axis=0, keepdims=True)
        value = (forward[k] - known) * inverse[k]
        solved = jnp.where(level == k, value, solved)
    return solved


def spread_out(values, rows, cols):
    down, right = rows - values.shape[0], cols - values.shape[1]
    return jnp.pad(values, ((0, down), (0, right)))


def as_column(row):
    return jnp.broadcast_to(row, (LANES, row.shape[1])).T


def detrend_kernel(
    obj_n, ep_n, order, near, lc_ref, valid_ref, pixel_ref, sigma_ref, modes_ref,
    jitter_ref, freq_ref, resid_ref, power_ref, basis_s, times_s,
    coef_s, modes_s, pix_send, pix_recv, ep_send, ep_recv, gram_send, gram_recv,
    mode_send, mode_recv, half_send, half_recv,
    pix_sem, ep_sem, gram_sem, mode_sem, half_sem,
):
    me_o, me_e = lax.axis_index("obj"), lax.axis_index("ep")
    rows, cols = lc_ref.shape
    blocks = cols // SUB
    share = rows // ep_n

    def device(do, de):
        return {
            "obj": lax.rem(me_o + do, obj_n),
            "ep": lax.rem(me_e + de, ep_n),
        }

    peers = list(near)
    peers += [(do, 0) for do in range(1, obj_n) if (do, 0) not in near]
    barrier = pltpu.get_barrier_semaphore()
    for do, de in peers:
        pl.semaphore_signal(barrier, inc=1, device_id=device(do, de), device_id_type=MESH)
    pl.semaphore_wait(barrier, len(peers))

    def sends_to(do):
        return None if do == 0 else me_o < obj_n - 1 if do == 1 else me_o > 0

    def hears_from(do):
        return None if do == 0 else me_o > 0 if do == 1 else me_o < obj_n - 1

    def guarded(condition, action):
        if condition is None:
            action()
        else:
            pl.when(condition)(action)

    for k, (do, de) in enumerate(near):
        if do != 0:
            @pl.when(jnp.logical_not(hears_from(do)))
            def _():
                pix_recv[:, k] = jnp.zeros(pix_recv.shape[:1] + pix_recv.shape[2:], F32)

    mask = valid_ref[...].astype(F32)
    sigma = as_column(sigma_ref[...])[:, :1]
    epochs = jitter_ref.shape[1]
    times_s[...] = as_column(
        lax.broadcasted_iota(jnp.int32, (1, epochs), 1).astype(F32) + jitter_ref[...]
    )
    width = basis_s.shape[3]

    def fill_basis(block):
        begin = pl.multiple_of(block * width, width)
        freqs = (freq_ref[:, pl.ds(begin, width)] + 1).astype(F32) / (4.0 * epochs)

        def strip(step, carry):
            at = pl.ds(pl.multiple_of(step * STRIP, STRIP), STRIP)
            times = jnp.concatenate([times_s[at, :]] * (width // LANES), axis=1)
            for kind, values in enumerate(basis_of(times * freqs)):
                basis_s[block, kind, at, :] = values.astype(jnp.bfloat16)
            return carry

        lax.fori_loop(0, epochs // STRIP, strip, 0)

    pixels = lax.broadcasted_iota(jnp.int32, (rows, pix_send.shape[2]), 1)
    member = (as_column(pixel_ref[...].astype(F32))[:, :1] == pixels.astype(F32)).astype(F32)
    counts = jnp.sum(member * jnp.sum(mask, axis=1, keepdims=True), axis=0, keepdims=True)

    def residual():
        return lc_ref[...] - lax.dot_general(
            coef_s[...], modes_s[...], (((0,), (0,)), ((), ())),
            precision=HIGHEST, preferred_element_type=F32,
        )

    def robust(resid, phase, block=None):
        scaled = resid * sigma
        squares = jnp.sum(mask * scaled * scaled, axis=1, keepdims=True)
        sums = jnp.sum(member * squares, axis=0, keepdims=True)
        part = spread_out(jnp.concatenate([sums, counts], axis=0), SUB, sums.shape[1])
        pix_send[phase] = part
        copies = []
        for k, (do, de) in enumerate(near):
            copies.append(pltpu.make_async_remote_copy(
                src_ref=pix_send.at[phase], dst_ref=pix_recv.at[phase, k],
                send_sem=pix_sem.at[0, phase, k], recv_sem=pix_sem.at[1, phase, k],
                device_id=device(do, de), device_id_type=MESH,
            ))
            guarded(sends_to(do), copies[k].start)
        if block is not None:
            fill_basis(block)
        for k, (do, de) in enumerate(near):
            guarded(sends_to(do), copies[k].wait_send)
            guarded(hears_from(do), copies[k].wait_recv)
        totals = part
        for k in range(len(near)):
            totals = totals + pix_recv[phase, k]
        spread = jnp.sqrt(totals[0:1] / jnp.maximum(totals[1:2], 1.0) + 1e-06)
        object_spread = jnp.sum(member * spread, axis=1, keepdims=True)
        zscore = scaled / object_spread
        huber = HUBER / jnp.maximum(jnp.abs(zscore), HUBER)
        return mask * huber * (sigma * sigma)

    coef_s[...] = jnp.zeros_like(coef_s)
    modes_s[...] = modes_ref[...]

    def iteration(it, carry):
        light = lc_ref[...]
        weight = robust(residual(), 2 * it, 4 * it)
        modes_t = modes_s[...]
        last = (((1,), (1,)), ((), ()))
        gram = lax.dot_general(
            packed_outer(modes_t), weight, last, precision=HIGHEST, preferred_element_type=F32
        )
        target = lax.dot_general(
            modes_t, weight * light, last, precision=HIGHEST, preferred_element_type=F32
        )
        packed = jnp.concatenate([gram, target], axis=0)
        ep_send[it] = packed
        copies = []
        for k in range(1, ep_n):
            copies.append(pltpu.make_async_remote_copy(
                src_ref=ep_send.at[it], dst_ref=ep_recv.at[it, k - 1],
                send_sem=ep_sem.at[0, it, k - 1], recv_sem=ep_sem.at[1, it, k - 1],
                device_id=device(0, k), device_id_type=MESH,
            ))
            copies[-1].start()
        for k in range(1, ep_n):
            copies[k - 1].wait()
            packed = packed + ep_recv[it, k - 1]
        coef_t = damped_solve(packed, order)
        coef_s[...] = coef_t

        weight = robust(residual(), 2 * it + 1, 4 * it + 1)
        gram = jnp.dot(
            packed_outer(coef_t), weight, precision=HIGHEST, preferred_element_type=F32
        )
        target = jnp.dot(
            coef_t, weight * light, precision=HIGHEST, preferred_element_type=F32
        )
        packed = jnp.concatenate([gram, target], axis=0)
        depth = packed.shape[0]
        wide = gram_send.shape[3]
        turned = spread_out(packed, wide, cols).T
        gram_send[it] = turned.reshape(blocks, SUB, wide)
        copies = []
        for k in range(1, obj_n):
            there = lax.rem(me_o + k, obj_n)
            copies.append(pltpu.make_async_remote_copy(
                src_ref=gram_send.at[it, lax.rem(there, blocks)],
                dst_ref=gram_recv.at[it, k - 1],
                send_sem=gram_sem.at[0, it, k - 1], recv_sem=gram_sem.at[1, it, k - 1],
                device_id=device(k, 0), device_id_type=MESH,
            ))
            copies[-1].start()
        fill_basis(4 * it + 2)
        total = gram_send[it, lax.rem(me_o, blocks)]
        for k in range(1, obj_n):
            copies[k - 1].wait()
            total = total + gram_recv[it, k - 1]
        packed = spread_out(total, LANES, wide).T[:depth]
        solved = damped_solve(packed, order)
        mine = spread_out(solved, LANES, LANES).T[:SUB]
        mode_send[it] = mine
        mode_recv[it, me_o] = mine
        copies = []
        for k in range(1, obj_n):
            copies.append(pltpu.make_async_remote_copy(
                src_ref=mode_send.at[it], dst_ref=mode_recv.at[it, me_o],
                send_sem=mode_sem.at[0, it, k - 1], recv_sem=mode_sem.at[1, it, k - 1],
                device_id=device(k, 0), device_id_type=MESH,
            ))
            copies[-1].start()
        fill_basis(4 * it + 3)
        for copy in copies:
            copy.wait()
        modes_s[...] = mode_recv[it, :blocks].reshape(cols, LANES).T[:order]
        return carry

    lax.fori_loop(0, ITERS, iteration, 0)
    resid = residual()
    resid_ref[...] = resid
    weight = robust(resid, 2 * ITERS)
    half_send[0] = (weight * resid).astype(jnp.bfloat16)
    half_send[1] = weight.astype(jnp.bfloat16)
    copies = []
    for k in range(1, ep_n):
        there = lax.rem(me_e + k, ep_n)
        copies.append(pltpu.make_async_remote_copy(
            src_ref=half_send.at[:, pl.ds(pl.multiple_of(there * share, share), share), :],
            dst_ref=half_recv.at[me_e],
            send_sem=half_sem.at[0, k - 1], recv_sem=half_sem.at[1, k - 1],
            device_id=device(0, k), device_id_type=MESH,
        ))
        copies[-1].start()
    half_recv[me_e] = half_send[:, pl.ds(pl.multiple_of(me_e * share, share), share), :]
    for copy in copies:
        copy.wait()
    received = [half_recv[e] for e in range(ep_n)]
    values = jnp.concatenate([half[0] for half in received], axis=1)
    weights = jnp.concatenate([half[1] for half in received], axis=1)
    both = jnp.concatenate([weights, values], axis=0)
    total = jnp.sum(weights.astype(F32), axis=1, keepdims=True)
    level = jnp.sum(values.astype(F32), axis=1, keepdims=True)

    def spectrum(block, carry):
        at = pl.ds(pl.multiple_of(block * width, width), width)
        power_ref[:, at] = powers(
            jnp.dot(both, basis_s[block, 0], preferred_element_type=F32),
            jnp.dot(both, basis_s[block, 1], preferred_element_type=F32),
            jnp.dot(weights, basis_s[block, 2], preferred_element_type=F32),
            jnp.dot(weights, basis_s[block, 3], preferred_element_type=F32),
            total,
            level,
        )
        return carry

    lax.fori_loop(0, basis_s.shape[0], spectrum, 0)


SIN_TERMS = [(-1.0) ** n / math.factorial(2 * n + 1) for n in range(7)]
COS_TERMS = [(-1.0) ** n / math.factorial(2 * n) for n in range(8)]


def series(square, terms):
    value = jnp.full_like(square, terms[-1])
    for term in terms[-2::-1]:
        value = value * square + term
    return value


def basis_of(cycles):
    cycles = cycles - jnp.floor(cycles)
    turn = jnp.where(cycles >= 0.5, cycles - 1.0, cycles)
    angle = (2.0 * math.pi) * (jnp.abs(turn) - 0.25)
    square = angle * angle
    cosine = -angle * series(square, SIN_TERMS)
    size = series(square, COS_TERMS)
    sine = jnp.where(turn < 0.0, -size, size)
    return cosine, sine, 2.0 * cosine * cosine - 1.0, 2.0 * sine * cosine


def powers(by_cos, by_sin, cosine_two, sine_two, total, level):
    count = cosine_two.shape[0]
    cosine, sine = by_cos[:count], by_sin[:count]
    inverse = 1.0 / total
    mean_level = level * inverse
    ycos = by_cos[count:] - mean_level * cosine
    ysin = by_sin[count:] - mean_level * sine
    cc_term = 0.5 * (total + cosine_two) - cosine * cosine * inverse + RIDGE * total
    ss_term = 0.5 * (total - cosine_two) - sine * sine * inverse + RIDGE * total
    cs_term = 0.5 * sine_two - cosine * sine * inverse
    determinant = cc_term * ss_term - cs_term * cs_term
    return (
        ss_term * ycos * ycos + cc_term * ysin * ysin - 2.0 * cs_term * ycos * ysin
    ) / determinant


def per_device(light_curves, valid, pixel, inv_sigma, modes_init, epoch_jitter, freq_index):
    obj_n = lax.axis_size("obj")
    ep_n = lax.axis_size("ep")
    order = modes_init.shape[1]
    rows, cols = light_curves.shape
    share = rows // ep_n
    epochs = epoch_jitter.shape[0]
    pix_lanes = -(-4 * obj_n // LANES) * LANES
    near = [
        (do, de)
        for do in sorted({0, 1 % obj_n, (obj_n - 1) % obj_n}, reverse=True)
        for de in reversed(range(ep_n))
        if (do, de) != (0, 0)
    ]
    depth = sum(order - first_of(i) for i in range(order)) + order
    wide = -(-depth // LANES) * LANES
    phases = 2 * ITERS + 1
    vmem = pl.BlockSpec(memory_space=pltpu.VMEM)
    sem = pltpu.SemaphoreType.DMA
    count = freq_index.shape[0]
    parts = 4 * ITERS
    return pl.pallas_call(
        functools.partial(detrend_kernel, obj_n, ep_n, order, near),
        out_shape=(
            jax.ShapeDtypeStruct((rows, cols), F32),
            jax.ShapeDtypeStruct((share, count), F32),
        ),
        in_specs=[vmem] * 7,
        out_specs=(vmem,) * 2,
        scratch_shapes=[
            pltpu.VMEM((parts, 4, epochs, count // parts), jnp.bfloat16),
            pltpu.VMEM((epochs, LANES), F32),
            pltpu.VMEM((order, rows), F32),
            pltpu.VMEM((order, cols), F32),
            pltpu.VMEM((phases, SUB, pix_lanes), F32),
            pltpu.VMEM((phases, len(near), SUB, pix_lanes), F32),
            pltpu.VMEM((ITERS, depth, rows), F32),
            pltpu.VMEM((ITERS, max(ep_n - 1, 1), depth, rows), F32),
            pltpu.VMEM((ITERS, cols // SUB, SUB, wide), F32),
            pltpu.VMEM((ITERS, max(obj_n - 1, 1), SUB, wide), F32),
            pltpu.VMEM((ITERS, SUB, LANES), F32),
            pltpu.VMEM((ITERS, max(obj_n, cols // SUB), SUB, LANES), F32),
            pltpu.VMEM((2, rows, cols), jnp.bfloat16),
            pltpu.VMEM((ep_n, 2, share, cols), jnp.bfloat16),
            sem((2, phases, len(near))),
            sem((2, ITERS, max(ep_n - 1, 1))),
            sem((2, ITERS, max(obj_n - 1, 1))),
            sem((2, ITERS, max(obj_n - 1, 1))),
            sem((2, max(ep_n - 1, 1))),
        ],
        compiler_params=pltpu.CompilerParams(collective_id=0, has_side_effects=True),
    )(
        light_curves, valid, pixel[None], inv_sigma[None], modes_init.T,
        epoch_jitter[None], freq_index[None],
    )


def solution(mesh):
    in_specs = (P("obj", "ep"), P("obj", "ep"), P("obj"), P("obj"), P("ep", None), P(), P())
    out_specs = (P("obj", "ep"), P(("obj", "ep"), None))
    return jax.shard_map(
        per_device, mesh=mesh, in_specs=in_specs, out_specs=out_specs, check_vma=False
    )
```

```python
import functools
import math

import jax
import jax.numpy as jnp
from jax import lax
from jax.experimental import pallas as pl
from jax.experimental.pallas import tpu as pltpu
from jax.sharding import PartitionSpec as P

ITERS = 2


HUBER = 1.345
DAMP = 2.0
RIDGE = 0.05
HIGHEST = lax.Precision.HIGHEST
LANES = 128
SUB = 8
F32 = jnp.float32
STRIP = 32
MESH = pl.DeviceIdType.MESH


def first_of(row):
    return SUB * (row // SUB)


def packed_outer(vectors):
    order = vectors.shape[0]
    return jnp.concatenate(
        [vectors[i : i + 1] * vectors[first_of(i) :] for i in range(order)], axis=0
    )


def damped_solve(packed, order):
    level = lax.broadcasted_iota(jnp.int32, (order, packed.shape[1]), 0)
    rows = []
    at = 0
    for i in range(order):
        low = first_of(i)
        rows.append(packed[at : at + order - low] + DAMP * (level[low:] == i).astype(F32))
        at += order - low
    remain = packed[at : at + order]
    inverse, forward = [], []
    for k in range(order):
        low = first_of(k)
        row = rows[k]
        inverse.append(1.0 / row[k - low : k - low + 1])
        scaled = row * inverse[k]
        for j in range(k + 1, order):
            begin = first_of(j)
            rows[j] = rows[j] - scaled[j - low : j - low + 1] * row[begin - low :]
        forward.append(remain[k : k + 1])
        part = remain[low:] - scaled * forward[k]
        remain = part if low == 0 else jnp.concatenate([remain[:low], part], axis=0)
    solved = jnp.zeros((order, packed.shape[1]), F32)
    for k in reversed(range(order)):
        low = first_of(k)
        known = jnp.sum(rows[k] * solved[low:], axis=0, keepdims=True)
        value = (forward[k] - known) * inverse[k]
        solved = jnp.where(level == k, value, solved)
    return solved


def spread_out(values, rows, cols):
    down, right = rows - values.shape[0], cols - values.shape[1]
    return jnp.pad(values, ((0, down), (0, right)))


def as_column(row):
    return jnp.broadcast_to(row, (LANES, row.shape[1])).T


def detrend_kernel(
    obj_n, ep_n, order, near, lc_ref, valid_ref, pixel_ref, sigma_ref, modes_ref,
    jitter_ref, freq_ref, resid_ref, power_ref, basis_s, times_s,
    coef_s, modes_s, pix_send, pix_recv, ep_send, ep_recv, gram_send, gram_recv,
    mode_send, mode_recv, half_send, half_recv,
    pix_sem, ep_sem, gram_sem, mode_sem, half_sem,
):
    me_o, me_e = lax.axis_index("obj"), lax.axis_index("ep")
    rows, cols = lc_ref.shape
    blocks = cols // SUB
    far = sorted(range(1, obj_n), key=lambda k: abs(2 * k - obj_n))
    share = rows // ep_n

    def device(do, de):
        return {
            "obj": lax.rem(me_o + do, obj_n),
            "ep": lax.rem(me_e + de, ep_n),
        }

    peers = list(near)
    peers += [(do, 0) for do in range(1, obj_n) if (do, 0) not in near]
    barrier = pltpu.get_barrier_semaphore()
    for do, de in peers:
        pl.semaphore_signal(barrier, inc=1, device_id=device(do, de), device_id_type=MESH)
    pl.semaphore_wait(barrier, len(peers))

    def sends_to(do):
        return None if do == 0 else me_o < obj_n - 1 if do == 1 else me_o > 0

    def hears_from(do):
        return None if do == 0 else me_o > 0 if do == 1 else me_o < obj_n - 1

    def guarded(condition, action):
        if condition is None:
            action()
        else:
            pl.when(condition)(action)

    for k, (do, de) in enumerate(near):
        if do != 0:
            @pl.when(jnp.logical_not(hears_from(do)))
            def _():
                pix_recv[:, k] = jnp.zeros(pix_recv.shape[:1] + pix_recv.shape[2:], F32)

    mask = valid_ref[...].astype(F32)
    sigma = as_column(sigma_ref[...])[:, :1]
    epochs = jitter_ref.shape[1]
    times_s[...] = as_column(
        lax.broadcasted_iota(jnp.int32, (1, epochs), 1).astype(F32) + jitter_ref[...]
    )
    width = basis_s.shape[3]

    def fill_basis(block):
        begin = pl.multiple_of(block * width, width)
        freqs = (freq_ref[:, pl.ds(begin, width)] + 1).astype(F32) / (4.0 * epochs)

        def strip(step, carry):
            at = pl.ds(pl.multiple_of(step * STRIP, STRIP), STRIP)
            times = jnp.concatenate([times_s[at, :]] * (width // LANES), axis=1)
            for kind, values in enumerate(basis_of(times * freqs)):
                basis_s[block, kind, at, :] = values.astype(jnp.bfloat16)
            return carry

        lax.fori_loop(0, epochs // STRIP, strip, 0)

    pixels = lax.broadcasted_iota(jnp.int32, (rows, pix_send.shape[2]), 1)
    member = (as_column(pixel_ref[...].astype(F32))[:, :1] == pixels.astype(F32)).astype(F32)
    counts = jnp.sum(member * jnp.sum(mask, axis=1, keepdims=True), axis=0, keepdims=True)

    def residual():
        return lc_ref[...] - lax.dot_general(
            coef_s[...], modes_s[...], (((0,), (0,)), ((), ())),
            precision=HIGHEST, preferred_element_type=F32,
        )

    def robust(resid, phase, block=None):
        scaled = resid * sigma
        squares = jnp.sum(mask * scaled * scaled, axis=1, keepdims=True)
        sums = jnp.sum(member * squares, axis=0, keepdims=True)
        part = spread_out(jnp.concatenate([sums, counts], axis=0), SUB, sums.shape[1])
        pix_send[phase] = part
        copies = []
        for k, (do, de) in enumerate(near):
            copies.append(pltpu.make_async_remote_copy(
                src_ref=pix_send.at[phase], dst_ref=pix_recv.at[phase, k],
                send_sem=pix_sem.at[0, phase, k], recv_sem=pix_sem.at[1, phase, k],
                device_id=device(do, de), device_id_type=MESH,
            ))
            guarded(sends_to(do), copies[k].start)
        if block is not None:
            fill_basis(block)
        for k, (do, de) in enumerate(near):
            guarded(sends_to(do), copies[k].wait_send)
            guarded(hears_from(do), copies[k].wait_recv)
        totals = part
        for k in range(len(near)):
            totals = totals + pix_recv[phase, k]
        spread = jnp.sqrt(totals[0:1] / jnp.maximum(totals[1:2], 1.0) + 1e-06)
        object_spread = jnp.sum(member * spread, axis=1, keepdims=True)
        zscore = scaled / object_spread
        huber = HUBER / jnp.maximum(jnp.abs(zscore), HUBER)
        return mask * huber * (sigma * sigma)

    coef_s[...] = jnp.zeros_like(coef_s)
    modes_s[...] = modes_ref[...]

    def iteration(it, carry):
        light = lc_ref[...]
        weight = robust(residual(), 2 * it, 4 * it)
        modes_t = modes_s[...]
        last = (((1,), (1,)), ((), ()))
        gram = lax.dot_general(
            packed_outer(modes_t), weight, last, precision=HIGHEST, preferred_element_type=F32
        )
        target = lax.dot_general(
            modes_t, weight * light, last, precision=HIGHEST, preferred_element_type=F32
        )
        packed = jnp.concatenate([gram, target], axis=0)
        ep_send[it] = packed
        copies = []
        for k in range(1, ep_n):
            copies.append(pltpu.make_async_remote_copy(
                src_ref=ep_send.at[it], dst_ref=ep_recv.at[it, k - 1],
                send_sem=ep_sem.at[0, it, k - 1], recv_sem=ep_sem.at[1, it, k - 1],
                device_id=device(0, k), device_id_type=MESH,
            ))
            copies[-1].start()
        for k in range(1, ep_n):
            copies[k - 1].wait()
            packed = packed + ep_recv[it, k - 1]
        coef_t = damped_solve(packed, order)
        coef_s[...] = coef_t

        weight = robust(residual(), 2 * it + 1, 4 * it + 1)
        gram = jnp.dot(
            packed_outer(coef_t), weight, precision=HIGHEST, preferred_element_type=F32
        )
        target = jnp.dot(
            coef_t, weight * light, precision=HIGHEST, preferred_element_type=F32
        )
        packed = jnp.concatenate([gram, target], axis=0)
        depth = packed.shape[0]
        wide = gram_send.shape[3]
        turned = spread_out(packed, wide, cols).T
        gram_send[it] = turned.reshape(blocks, SUB, wide)
        copies = []
        for k in far:
            there = lax.rem(me_o + k, obj_n)
            copies.append(pltpu.make_async_remote_copy(
                src_ref=gram_send.at[it, lax.rem(there, blocks)],
                dst_ref=gram_recv.at[it, k - 1],
                send_sem=gram_sem.at[0, it, k - 1], recv_sem=gram_sem.at[1, it, k - 1],
                device_id=device(k, 0), device_id_type=MESH,
            ))
            copies[-1].start()
        fill_basis(4 * it + 2)
        total = gram_send[it, lax.rem(me_o, blocks)]
        for k, copy in zip(far, copies):
            copy.wait()
            total = total + gram_recv[it, k - 1]
        packed = spread_out(total, LANES, wide).T[:depth]
        solved = damped_solve(packed, order)
        mine = spread_out(solved, LANES, LANES).T[:SUB]
        mode_send[it] = mine
        mode_recv[it, me_o] = mine
        copies = []
        for k in far:
            copies.append(pltpu.make_async_remote_copy(
                src_ref=mode_send.at[it], dst_ref=mode_recv.at[it, me_o],
                send_sem=mode_sem.at[0, it, k - 1], recv_sem=mode_sem.at[1, it, k - 1],
                device_id=device(k, 0), device_id_type=MESH,
            ))
            copies[-1].start()
        fill_basis(4 * it + 3)
        for copy in copies:
            copy.wait()
        modes_s[...] = mode_recv[it, :blocks].reshape(cols, LANES).T[:order]
        return carry

    lax.fori_loop(0, ITERS, iteration, 0)
    resid = residual()
    resid_ref[...] = resid
    weight = robust(resid, 2 * ITERS)
    half_send[0] = (weight * resid).astype(jnp.bfloat16)
    half_send[1] = weight.astype(jnp.bfloat16)
    copies = []
    for k in range(1, ep_n):
        there = lax.rem(me_e + k, ep_n)
        copies.append(pltpu.make_async_remote_copy(
            src_ref=half_send.at[:, pl.ds(pl.multiple_of(there * share, share), share), :],
            dst_ref=half_recv.at[me_e],
            send_sem=half_sem.at[0, k - 1], recv_sem=half_sem.at[1, k - 1],
            device_id=device(0, k), device_id_type=MESH,
        ))
        copies[-1].start()
    half_recv[me_e] = half_send[:, pl.ds(pl.multiple_of(me_e * share, share), share), :]
    for copy in copies:
        copy.wait()
    received = [half_recv[e] for e in range(ep_n)]
    values = jnp.concatenate([half[0] for half in received], axis=1)
    weights = jnp.concatenate([half[1] for half in received], axis=1)
    both = jnp.concatenate([weights, values], axis=0)
    total = jnp.sum(weights.astype(F32), axis=1, keepdims=True)
    level = jnp.sum(values.astype(F32), axis=1, keepdims=True)

    def spectrum(block, carry):
        at = pl.ds(pl.multiple_of(block * width, width), width)
        power_ref[:, at] = powers(
            jnp.dot(both, basis_s[block, 0], preferred_element_type=F32),
            jnp.dot(both, basis_s[block, 1], preferred_element_type=F32),
            jnp.dot(weights, basis_s[block, 2], preferred_element_type=F32),
            jnp.dot(weights, basis_s[block, 3], preferred_element_type=F32),
            total,
            level,
        )
        return carry

    lax.fori_loop(0, basis_s.shape[0], spectrum, 0)


SIN_TERMS = [(-1.0) ** n / math.factorial(2 * n + 1) for n in range(7)]
COS_TERMS = [(-1.0) ** n / math.factorial(2 * n) for n in range(8)]


def series(square, terms):
    value = jnp.full_like(square, terms[-1])
    for term in terms[-2::-1]:
        value = value * square + term
    return value


def basis_of(cycles):
    cycles = cycles - jnp.floor(cycles)
    turn = jnp.where(cycles >= 0.5, cycles - 1.0, cycles)
    angle = (2.0 * math.pi) * (jnp.abs(turn) - 0.25)
    square = angle * angle
    cosine = -angle * series(square, SIN_TERMS)
    size = series(square, COS_TERMS)
    sine = jnp.where(turn < 0.0, -size, size)
    return cosine, sine, 2.0 * cosine * cosine - 1.0, 2.0 * sine * cosine


def powers(by_cos, by_sin, cosine_two, sine_two, total, level):
    count = cosine_two.shape[0]
    cosine, sine = by_cos[:count], by_sin[:count]
    inverse = 1.0 / total
    mean_level = level * inverse
    ycos = by_cos[count:] - mean_level * cosine
    ysin = by_sin[count:] - mean_level * sine
    cc_term = 0.5 * (total + cosine_two) - cosine * cosine * inverse + RIDGE * total
    ss_term = 0.5 * (total - cosine_two) - sine * sine * inverse + RIDGE * total
    cs_term = 0.5 * sine_two - cosine * sine * inverse
    determinant = cc_term * ss_term - cs_term * cs_term
    return (
        ss_term * ycos * ycos + cc_term * ysin * ysin - 2.0 * cs_term * ycos * ysin
    ) / determinant


def per_device(light_curves, valid, pixel, inv_sigma, modes_init, epoch_jitter, freq_index):
    obj_n = lax.axis_size("obj")
    ep_n = lax.axis_size("ep")
    order = modes_init.shape[1]
    rows, cols = light_curves.shape
    share = rows // ep_n
    epochs = epoch_jitter.shape[0]
    pix_lanes = -(-4 * obj_n // LANES) * LANES
    near = [
        (do, de)
        for do in sorted({0, 1 % obj_n, (obj_n - 1) % obj_n}, reverse=True)
        for de in reversed(range(ep_n))
        if (do, de) != (0, 0)
    ]
    depth = sum(order - first_of(i) for i in range(order)) + order
    wide = -(-depth // LANES) * LANES
    phases = 2 * ITERS + 1
    vmem = pl.BlockSpec(memory_space=pltpu.VMEM)
    sem = pltpu.SemaphoreType.DMA
    count = freq_index.shape[0]
    parts = 4 * ITERS
    return pl.pallas_call(
        functools.partial(detrend_kernel, obj_n, ep_n, order, near),
        out_shape=(
            jax.ShapeDtypeStruct((rows, cols), F32),
            jax.ShapeDtypeStruct((share, count), F32),
        ),
        in_specs=[vmem] * 7,
        out_specs=(vmem,) * 2,
        scratch_shapes=[
            pltpu.VMEM((parts, 4, epochs, count // parts), jnp.bfloat16),
            pltpu.VMEM((epochs, LANES), F32),
            pltpu.VMEM((order, rows), F32),
            pltpu.VMEM((order, cols), F32),
            pltpu.VMEM((phases, SUB, pix_lanes), F32),
            pltpu.VMEM((phases, len(near), SUB, pix_lanes), F32),
            pltpu.VMEM((ITERS, depth, rows), F32),
            pltpu.VMEM((ITERS, max(ep_n - 1, 1), depth, rows), F32),
            pltpu.VMEM((ITERS, cols // SUB, SUB, wide), F32),
            pltpu.VMEM((ITERS, max(obj_n - 1, 1), SUB, wide), F32),
            pltpu.VMEM((ITERS, SUB, LANES), F32),
            pltpu.VMEM((ITERS, max(obj_n, cols // SUB), SUB, LANES), F32),
            pltpu.VMEM((2, rows, cols), jnp.bfloat16),
            pltpu.VMEM((ep_n, 2, share, cols), jnp.bfloat16),
            sem((2, phases, len(near))),
            sem((2, ITERS, max(ep_n - 1, 1))),
            sem((2, ITERS, max(obj_n - 1, 1))),
            sem((2, ITERS, max(obj_n - 1, 1))),
            sem((2, max(ep_n - 1, 1))),
        ],
        compiler_params=pltpu.CompilerParams(collective_id=0, has_side_effects=True),
    )(
        light_curves, valid, pixel[None], inv_sigma[None], modes_init.T,
        epoch_jitter[None], freq_index[None],
    )


def solution(mesh):
    in_specs = (P("obj", "ep"), P("obj", "ep"), P("obj"), P("obj"), P("ep", None), P(), P())
    out_specs = (P("obj", "ep"), P(("obj", "ep"), None))
    return jax.shard_map(
        per_device, mesh=mesh, in_specs=in_specs, out_specs=out_specs, check_vma=False
    )
```
